32 devices in a mesh: pipe: 2 (over y), expert: 16 (over z, x, core).
Axes of the slice: x: 2, y: 2, z: 4, core: 2. Of those that a mesh axis runs over, the one named last changes fastest.
Arguments:
- resident_batchlets: bfloat16 [2, 256, 2048], P('pipe', 'expert'), may hold values from -6 to 6
- incoming_batchlets: bfloat16 [1, 256, 2048], P(None, 'expert'), may hold values from -6 to 6
- segment_rms_gain: float32 [2, 2048], P('pipe'), may hold values from 0.25 to 1.75
- gating_projection: bfloat16 [16, 2048, 768], P('expert'), may hold values from -0.125 to 0.125
- expanding_projection: bfloat16 [16, 2048, 768], P('expert'), may hold values from -0.125 to 0.125
- contracting_projection: bfloat16 [16, 768, 2048], P('expert'), may hold values from -0.21875 to 0.21875
- picked_specialist_ids: int32 [2, 2, 256, 8], P(None, 'pipe', 'expert'), may hold values from 0 to 15, all different within a row; in each aligned block of 16 rows (0 to 15, 16 to 31, ..., all dimensions but the last counted through in order) at most 9 rows name the same one
- blend_factors: float32 [2, 2, 256, 8], P(None, 'pipe', 'expert'), may hold values from 0.02 to 0.25
Outputs:
- stash: bfloat16 [2, 2, 256, 2048], P(None, 'pipe', 'expert')
The draws below stay inside these ranges and needn't reach their ends.
Inputs may be any that keep to these rules, and one draw needn't show every extreme that they name: `picked_specialist_ids`: each row names 8 different experts. Among the rows of one device (aligned blocks of 16 rows), no expert is named more than 9 times, and in some blocks one expert is named exactly 9 times.
All inputs are finite; a program needn't handle non-finite values.
Results may differ from the reference program's by a relative error of at most 0.005.
Values may be sent and summed in bfloat16 or wider, within the bound.
No kernel may reach another device: no remote copies, remote signals or barrier semaphores. Data moves between devices by JAX's collectives and lax.ppermute only.
A program may use at most 64 MiB of HBM per device.

```python
import math
import jax
import jax.numpy as jnp
import numpy as np
from jax import lax

HIDDEN_FEATURES = 2048
FF = 768
TOP = 8
TICKS = 2
TOK_DEV = 16
EXPERTS = 16
BATCHLET_ITEMS = 256
C_SRC = 9
FEEDS = 1
N_PIPE = 2
N_EXPERT = 16


def levels(rng, shape, cuts, least, largest):
    def one(position, blocks):
        draws = jax.random.uniform(jax.random.fold_in(jax.random.fold_in(rng, 6), position), (blocks,), jnp.float32, least / len(cuts), largest / len(cuts))
        return jnp.repeat(jnp.exp(draws), shape[position] // blocks).reshape((-1,) + (1,) * (len(shape) - position - 1))

    level = one(*cuts[0])
    for cut in cuts[1:]:
        level = level * one(*cut)
    return level


def routed_block(stream_key, own, number, rows, amount, top, most, lean):
    order = jax.random.permutation(stream_key, amount)
    packed, ordinary = load_shares(amount, rows * top, most, lean, True), load_shares(amount, rows * top, most, lean, False)
    places = jnp.arange(amount)

    def named(sizes, turn):
        used = int((sizes > 0).sum())
        fixed = max(1, used // 4)
        moved = fixed + (places - fixed + turn * (used - fixed)) % max(1, amount - fixed)
        return jnp.zeros((amount,), jnp.int32).at[order[jnp.where(places < fixed, places, moved)]].set(jnp.asarray(sizes, jnp.int32))

    sizes = jnp.where(number % 4 == 0, named(packed, number // 4), named(ordinary, number - number // 4 - 1))
    mixed = jax.random.permutation(jax.random.fold_in(own, 3), amount)
    giver, taker = mixed[0:amount // 2 * 2:2], mixed[1:amount // 2 * 2:2]
    slack = jnp.minimum(sizes[giver] - 1, most - sizes[taker]) // 2
    slack = jnp.where((giver == order[0]) | (taker == order[0]) | (sizes[taker] == 0), 0, jnp.maximum(slack, 0))
    moved = jax.random.randint(jax.random.fold_in(own, 4), (amount // 2,), 0, 1 << 20) % (slack + 1)
    sizes = sizes.at[giver].add(-moved).at[taker].add(moved)
    labels = jnp.searchsorted(jnp.cumsum(sizes), jnp.arange(rows * top), side="right").astype(jnp.int32)
    grid = labels.reshape(top, rows).T
    grid = grid[jax.random.permutation(jax.random.fold_in(own, 1), rows)]
    turn = jax.random.randint(jax.random.fold_in(own, 2), (rows, 1), 0, top)
    return jnp.take_along_axis(grid, (jnp.arange(top)[None, :] + turn) % top, axis=1)


def load_shares(amount, total, most, slope, full):
    loads = [(1 << 20) // math.isqrt(grade ** slope) + 1 for grade in range(1, amount + 1)]
    largest = most if full else min(most, max(-(-total // amount), total * loads[0] // sum(loads)))
    least = 1 if total - largest >= amount - 1 else 0
    counts, surplus = [largest] + [least] * (amount - 1), total - largest - least * (amount - 1)
    while surplus > 0:
        movable = [i for i in range(1, amount) if counts[i] < largest] or [i for i in range(1, amount) if counts[i] < most]
        pool, budget = sum([loads[i] for i in movable]), surplus
        for i in movable:
            more = min(most - counts[i], max(1, budget * loads[i] // pool), surplus)
            counts[i] = counts[i] + more
            surplus = surplus - more
    return np.array(counts)


def centred(own_key, dims, width, reach, pieces=(), kind=jnp.bfloat16):
    loudness = levels(own_key, dims, pieces, -0.22, 0.18) if pieces else 1.0
    entries = jax.random.normal(own_key, dims, jnp.float32) * width * loudness
    return jnp.minimum(jnp.maximum(entries, -reach), reach).astype(kind)


def setup_inputs(seed: int = 0) -> dict:
    streams_of = jax.random.split(jax.random.key(seed), 9)
    resident_batchlets = centred(streams_of[0], (N_PIPE, BATCHLET_ITEMS, HIDDEN_FEATURES), 1.0, 6.0, ((0, 2), (1, 16)))
    incoming_batchlets = centred(streams_of[1], (FEEDS, BATCHLET_ITEMS, HIDDEN_FEATURES), 1.0, 6.0, ((1, 16),))
    segment_rms_gain = jnp.clip(1.0 + 0.15 * jax.random.normal(streams_of[2], (N_PIPE, HIDDEN_FEATURES), jnp.float32), 0.25, 1.75)
    gating_projection = centred(streams_of[3], (EXPERTS, HIDDEN_FEATURES, FF), HIDDEN_FEATURES ** -0.5, 0.125, ((0, 16),))
    expanding_projection = centred(streams_of[4], (EXPERTS, HIDDEN_FEATURES, FF), HIDDEN_FEATURES ** -0.5, 0.125, ((0, 16),))
    contracting_projection = centred(streams_of[5], (EXPERTS, FF, HIDDEN_FEATURES), FF ** -0.5, 0.21875, ((0, 16),))
    picked_specialist_ids_keys = jax.random.split(jax.random.fold_in(streams_of[6], 1), TICKS * N_PIPE * BATCHLET_ITEMS // TOK_DEV)
    picked_specialist_ids_turns = jax.random.permutation(jax.random.fold_in(streams_of[6], 3), TICKS * N_PIPE * BATCHLET_ITEMS // TOK_DEV)
    picked_specialist_ids = jax.vmap(lambda own, number: routed_block(jax.random.fold_in(streams_of[6], 2), own, number, TOK_DEV, EXPERTS, TOP, C_SRC, 2))(picked_specialist_ids_keys, picked_specialist_ids_turns).reshape((TICKS, N_PIPE, BATCHLET_ITEMS, TOP))
    blend_factors = jnp.clip(0.02 + 0.23 * jax.random.uniform(streams_of[7], (TICKS, N_PIPE, BATCHLET_ITEMS, TOP), jnp.float32) ** levels(streams_of[7], (TICKS, N_PIPE, BATCHLET_ITEMS, TOP), ((1, 2), (2, 16)), -0.2, 0.2), 0.02, 0.25)
    return dict(resident_batchlets=resident_batchlets, incoming_batchlets=incoming_batchlets, segment_rms_gain=segment_rms_gain, gating_projection=gating_projection, expanding_projection=expanding_projection, contracting_projection=contracting_projection, picked_specialist_ids=picked_specialist_ids, blend_factors=blend_factors)


epsilon = 1e-06

def normalize(hidden_rows, gain_row):
    values = hidden_rows.astype(jnp.float32)
    scale = lax.rsqrt(lax.optimization_barrier(jnp.mean(values * values, axis=-1, keepdims=True)) + epsilon)
    return (values * scale * gain_row).astype(jnp.bfloat16)

def swiglu(tile_rows, gate_matrix, up_matrix, down_matrix):
    gate_part = jnp.dot(tile_rows, gate_matrix, preferred_element_type=jnp.float32)
    up_part = jnp.dot(tile_rows, up_matrix, preferred_element_type=jnp.float32)
    inner = (jax.nn.silu(gate_part) * up_part).astype(jnp.bfloat16)
    return jnp.dot(inner, down_matrix, preferred_element_type=jnp.float32).astype(jnp.bfloat16)

def section_layer(carry_value, gain_row, gate_stack, up_stack, down_stack, chosen, mix_weights):
    normed = normalize(carry_value, gain_row)
    limit = N_EXPERT * C_SRC

    def visit(mixed_sum, operands):
        gate_matrix, up_matrix, down_matrix, expert_number = operands
        hits = chosen == expert_number
        present = jnp.any(hits, axis=1)
        members = jnp.nonzero(present, size=limit, fill_value=0)[0]
        valid = jnp.arange(limit) < jnp.sum(present.astype(jnp.int32))
        weight_rows = lax.optimization_barrier(jnp.sum(jnp.where(hits, mix_weights, jnp.zeros_like(mix_weights)), axis=1))
        picked = jnp.take(normed, members, axis=0)
        produced = swiglu(picked, gate_matrix, up_matrix, down_matrix)
        scaled = jnp.where(valid, jnp.take(weight_rows, members), jnp.zeros((limit,), jnp.float32))
        mixed_sum = mixed_sum.at[members].add(produced.astype(jnp.float32) * scaled[:, None])
        return (mixed_sum, None)
    start = jnp.zeros((carry_value.shape[0], carry_value.shape[1]), jnp.float32)
    numbers = jnp.arange(EXPERTS, dtype=jnp.int32)
    mixed_sum, unused = lax.scan(visit, start, (gate_stack, up_stack, down_stack, numbers))
    return (carry_value.astype(jnp.float32) + mixed_sum).astype(jnp.bfloat16)

def reference(resident_batchlets, incoming_batchlets, segment_rms_gain, gating_projection, expanding_projection, contracting_projection, picked_specialist_ids, blend_factors):

    def run_section(operands):
        return section_layer(operands[0], operands[1], gating_projection, expanding_projection, contracting_projection, operands[2], operands[3])
    carry_value = resident_batchlets
    outputs = []
    for moment in range(TICKS):
        stepped = lax.map(run_section, (carry_value, segment_rms_gain, picked_specialist_ids[moment], blend_factors[moment]))
        outputs.append(stepped)
        if moment + 1 < TICKS:
            carry_value = jnp.concatenate([incoming_batchlets[moment][None], stepped[:-1]], axis=0)
    return jnp.stack(outputs, axis=0)
```

```python
import functools

import jax
import jax.numpy as jnp
from jax import lax
from jax.experimental import pallas as pl
from jax.experimental.pallas import tpu as pltpu
from jax.sharding import PartitionSpec as P

epsilon = 1e-06
LANES = 128
VMEM = pl.BlockSpec(memory_space=pltpu.VMEM)
SMEM = pl.BlockSpec(memory_space=pltpu.SMEM)


def params(mib):
    return pltpu.CompilerParams(vmem_limit_bytes=mib << 20)


class Plan:
    def __init__(self, size):
        self.size = size
        self.ring = size // 4
        half = self.ring // 2
        pairs = []
        for side in (0, 1):
            for step in range(1, (self.ring + 1) // 2):
                pairs.append(((step, side), (-step, side)))
        if self.ring % 2 == 0:
            pairs.append(((half, 0), (half, 1)))
        self.core = [(i, i ^ 1) for i in range(size)]
        self.side = [(i, i ^ 2) for i in range(size)]
        self.far = [self.mixed(*pair) for pair in pairs]
        self.back = [[(b, a) for a, b in perm] for perm in self.far]

    def mixed(self, first, second):
        out = []
        for i in range(self.size):
            place, side, core = i // 4, (i // 2) % 2, i % 2
            step, flip = (first, second)[core]
            out.append((i, ((place + step) % self.ring) * 4 + (side ^ flip) * 2 + core))
        return out


def rms(values, gain_row):
    scale = lax.rsqrt(jnp.mean(values * values, axis=-1, keepdims=True) + epsilon)
    return (values * scale * gain_row).astype(jnp.bfloat16)


def first_kernel(experts, x_ref, gain_ref, ids_ref, blend_ref, out_ref):
    rows, features = x_ref.shape
    ticks, top = ids_ref.shape[0], ids_ref.shape[2]
    extra = out_ref.shape[1] - features
    out_ref[:, :features] = rms(x_ref[...].astype(jnp.float32), gain_ref[...])
    lane = lax.broadcasted_iota(jnp.int32, (rows, extra), 1)
    expert = lane % experts
    value = jnp.zeros((rows, extra), jnp.float32)
    for tick in range(ticks):
        ids = ids_ref[tick]
        blend = blend_ref[tick]
        mine = lane // (2 * experts) == tick
        for k in range(top):
            hit = jnp.logical_and(mine, expert == ids[:, k : k + 1])
            value = value + jnp.where(hit, blend[:, k : k + 1], 0.0)
    high = value.astype(jnp.bfloat16).astype(jnp.float32)
    low = value - high
    upper = (lane // experts) % 2 == 0
    out_ref[:, features:] = jnp.where(upper, high, low).astype(jnp.bfloat16)


def next_kernel(section_ref, fed_ref, passed_ref, gain_ref, out_ref, state_ref):
    state = jnp.where(section_ref[0] == 0, fed_ref[...].astype(jnp.float32), passed_ref[...].astype(jnp.float32))
    state_ref[...] = state.astype(jnp.bfloat16)
    out_ref[...] = rms(state, gain_ref[...])


def join_kernel(a_ref, b_ref, out_ref):
    rows = a_ref.shape[0]
    out_ref[:rows] = a_ref[...]
    out_ref[rows:] = b_ref[...]


def expert_kernel(tick, experts, pieces, mine_ref, *refs):
    blocks = refs[:pieces]
    refs = refs[pieces:]
    if tick:
        factor_ref, refs = refs[0], refs[1:]
        gate_ref, up_ref, down_ref, keep_ref, send_ref, rows_ref, inner_ref = refs
    else:
        gate_ref, up_ref, down_ref, keep_ref, send_ref, factor_ref, rows_ref, inner_ref = refs
    total, features = rows_ref.shape
    at = 0
    for block in blocks:
        count = block.shape[0]
        rows_ref[at : at + count] = block[:, :features]
        if not tick:
            factor_ref[at : at + count] = block[:, features:]
        at += count
    extra = factor_ref.shape[1]
    hidden = gate_ref.shape[1]
    step = min(256, total)
    wide = 256 if hidden % 256 == 0 else LANES
    tall = 512 if features % 512 == 0 else LANES
    half = total // 2

    @pl.loop(0, total // step)
    def _(part):
        span = pl.ds(pl.multiple_of(part * step, step), step)
        lane = lax.broadcasted_iota(jnp.int32, (step, extra), 1)
        wanted = jnp.logical_and(lane // (2 * experts) == tick, lane % experts == mine_ref[0])
        factor = jnp.sum(jnp.where(wanted, factor_ref[span].astype(jnp.float32), 0.0), axis=1, keepdims=True)
        rows = rows_ref[span]
        for tile in range(hidden // wide):
            cols = slice(tile * wide, (tile + 1) * wide)
            gate = jnp.dot(rows, gate_ref[:, cols], preferred_element_type=jnp.float32)
            up = jnp.dot(rows, up_ref[:, cols], preferred_element_type=jnp.float32)
            inner = gate / (1.0 + jnp.exp(-gate)) * up * factor
            inner_ref[span, cols] = inner.astype(jnp.bfloat16)

    for start, out_ref in ((0, keep_ref), (half, send_ref)):
        inner = inner_ref[start : start + half]
        for tile in range(features // tall):
            cols = slice(tile * tall, (tile + 1) * tall)
            out_ref[:, cols] = jnp.dot(inner, down_ref[:, cols], preferred_element_type=jnp.float32).astype(jnp.bfloat16)


def chip_kernel(keep_ref, got_ref, own_ref, side_ref, *far_refs):
    rows = own_ref.shape[0]
    total = keep_ref[...].astype(jnp.float32) + got_ref[...].astype(jnp.float32)
    own_ref[...] = total[:rows]
    side_ref[...] = total[rows : 2 * rows].astype(jnp.bfloat16)
    for j, far_ref in enumerate(far_refs):
        far_ref[...] = total[2 * rows * (j + 1) : 2 * rows * (j + 2)].astype(jnp.bfloat16)


def gather_kernel(count, x_ref, own_ref, side_ref, *refs):
    far_refs, (mine_ref, other_ref) = refs[:count], refs[count:]
    rows = x_ref.shape[0]
    total = far_refs[0][...].astype(jnp.float32)
    for far_ref in far_refs[1:]:
        total = total + far_ref[...].astype(jnp.float32)
    mine_ref[...] = x_ref[...].astype(jnp.float32) + own_ref[...] + side_ref[...].astype(jnp.float32) + total[:rows]
    other_ref[...] = total[rows:].astype(jnp.bfloat16)


def finish_kernel(mine_ref, got_ref, out_ref):
    out_ref[...] = (mine_ref[...] + got_ref[...].astype(jnp.float32)).astype(jnp.bfloat16)


def last_kernel(mine_ref, got_ref, *refs):
    earlier, out_ref = refs[:-1], refs[-1]
    for tick, ref in enumerate(earlier):
        out_ref[tick, 0] = ref[...]
    out_ref[len(earlier), 0] = (mine_ref[...] + got_ref[...].astype(jnp.float32)).astype(jnp.bfloat16)


def call(kernel, outs, *args, smem=0, scratch=(), mib=32):
    single = not isinstance(outs, (list, tuple))
    return pl.pallas_call(
        kernel,
        out_shape=outs,
        in_specs=[SMEM] * smem + [VMEM] * (len(args) - smem),
        out_specs=VMEM if single else [VMEM] * len(outs),
        scratch_shapes=list(scratch),
        compiler_params=params(mib),
    )(*args)


def shape(rows, columns, dtype=jnp.bfloat16):
    return jax.ShapeDtypeStruct((rows, columns), dtype)


def local(
    resident_batchlets,
    incoming_batchlets,
    segment_rms_gain,
    gating_projection,
    expanding_projection,
    contracting_projection,
    picked_specialist_ids,
    blend_factors,
):
    experts = lax.axis_size("expert")
    sections = lax.axis_size("pipe")
    plan = Plan(experts)
    mine = lax.axis_index("expert").astype(jnp.int32).reshape(1)
    section = lax.axis_index("pipe").astype(jnp.int32).reshape(1)
    rows, features = resident_batchlets.shape[1:]
    ticks = picked_specialist_ids.shape[0]
    extra = -(-2 * ticks * experts // LANES) * LANES
    weights = (gating_projection[0], expanding_projection[0], contracting_projection[0])
    hidden = weights[0].shape[1]
    total = rows * experts

    def move(value, perm):
        return lax.ppermute(value, "expert", perm)

    state = resident_batchlets[0]
    factors = None
    outputs = []
    for tick in range(ticks):
        if tick == 0:
            normed = call(
                functools.partial(first_kernel, experts),
                shape(rows, features + extra),
                state,
                segment_rms_gain,
                picked_specialist_ids[:, 0],
                blend_factors[:, 0],
            )
        else:
            passed = lax.ppermute(outputs[-1], "pipe", [(i, i + 1) for i in range(sections - 1)])
            normed, state = call(
                next_kernel,
                [shape(rows, features), shape(rows, features)],
                section,
                incoming_batchlets[tick - 1],
                passed,
                segment_rms_gain,
                smem=1,
            )
        width = normed.shape[1]
        beside = move(normed, plan.side)
        partner = move(normed, plan.core)
        chip = call(join_kernel, shape(2 * rows, width), normed, partner)
        far = [move(chip, perm) for perm in plan.far]
        direct = [normed, beside] + far
        relayed = [partner] + [move(block, plan.core) for block in direct[1:]]
        blocks = direct + relayed
        outs = [shape(total // 2, features), shape(total // 2, features)]
        if tick == 0:
            outs.append(shape(total, extra))
        args = [mine] + blocks + ([factors] if tick else []) + list(weights)
        got = call(
            functools.partial(expert_kernel, tick, experts, len(blocks)),
            outs,
            *args,
            smem=1,
            scratch=[pltpu.VMEM((total, features), jnp.bfloat16), pltpu.VMEM((total, hidden), jnp.bfloat16)],
            mib=48,
        )
        keep, send = got[:2]
        if tick == 0:
            factors = got[2]
        swapped = move(send, plan.core)
        own, side, *far = call(
            chip_kernel,
            [shape(rows, features, jnp.float32), shape(rows, features)] + [shape(2 * rows, features)] * len(plan.back),
            keep,
            swapped,
        )
        far = [move(block, perm) for block, perm in zip(far, plan.back)]
        side = move(side, plan.side)
        part, other = call(
            functools.partial(gather_kernel, len(far)),
            [shape(rows, features, jnp.float32), shape(rows, features)],
            state,
            own,
            side,
            *far,
        )
        other = move(other, plan.core)
        if tick + 1 < ticks:
            outputs.append(call(finish_kernel, shape(rows, features), part, other))
        else:
            return call(last_kernel, jax.ShapeDtypeStruct((ticks, 1, rows, features), jnp.bfloat16), part, other, *outputs)


def solution(mesh):
    in_specs = (
        P("pipe", "expert", None),
        P(None, "expert", None),
        P("pipe", None),
        P("expert", None, None),
        P("expert", None, None),
        P("expert", None, None),
        P(None, "pipe", "expert", None),
        P(None, "pipe", "expert", None),
    )
    out_specs = P(None, "pipe", "expert", None)
    return jax.shard_map(local, mesh=mesh, in_specs=in_specs, out_specs=out_specs, check_vma=False)
```

```python
import functools

import jax
import jax.numpy as jnp
from jax import lax
from jax.experimental import pallas as pl
from jax.experimental.pallas import tpu as pltpu
from jax.sharding import PartitionSpec as P

epsilon = 1e-06
LANES = 128
VMEM = pl.BlockSpec(memory_space=pltpu.VMEM)
HBM = pl.BlockSpec(memory_space=pltpu.HBM)
ANY = pl.BlockSpec(memory_space=pl.ANY)


def params(mib):
    return pltpu.CompilerParams(vmem_limit_bytes=mib << 20)


class Plan:
    def __init__(self, size):
        self.size = size
        self.ring = size // 4
        half = self.ring // 2
        pairs = []
        for side in (0, 1):
            for step in range(1, (self.ring + 1) // 2):
                pairs.append(((step, side), (-step, side)))
        if self.ring % 2 == 0:
            pairs.append(((half, 0), (half, 1)))
        self.core = [(i, i ^ 1) for i in range(size)]
        self.side = [(i, i ^ 2) for i in range(size)]
        self.far = [self.mixed(*pair) for pair in pairs]
        self.back = [[(b, a) for a, b in perm] for perm in self.far]

    def mixed(self, first, second):
        out = []
        for i in range(self.size):
            place, side, core = i // 4, (i // 2) % 2, i % 2
            step, flip = (first, second)[core]
            out.append((i, ((place + step) % self.ring) * 4 + (side ^ flip) * 2 + core))
        return out


def rms(values, gain_row):
    scale = lax.rsqrt(jnp.mean(values * values, axis=-1, keepdims=True) + epsilon)
    return (values * scale * gain_row).astype(jnp.bfloat16)


def column(row):
    count = row.shape[1]
    above = lax.broadcasted_iota(jnp.int32, (count, count), 0)
    across = lax.broadcasted_iota(jnp.int32, (count, count), 1)
    return jnp.sum(jnp.where(above == across, row, jnp.zeros_like(row)), axis=1, keepdims=True)


def first_kernel(experts, x_hbm, gain_hbm, ids_hbm, blend_hbm, out_ref, state_ref, gain_ref, ids_ref, blend_ref, sems):
    pairs = ((x_hbm, state_ref), (gain_hbm, gain_ref), (ids_hbm, ids_ref), (blend_hbm, blend_ref))
    copies = [pltpu.make_async_copy(a, b, sems.at[i]) for i, (a, b) in enumerate(pairs)]
    for copy in copies:
        copy.start()
    for copy in copies:
        copy.wait()
    rows, features = state_ref.shape
    ticks, top = ids_ref.shape[0], ids_ref.shape[1]
    extra = out_ref.shape[1] - features
    out_ref[:, :features] = rms(state_ref[...].astype(jnp.float32), gain_ref[...])
    lane = lax.broadcasted_iota(jnp.int32, (rows, extra), 1)
    expert = lane % experts
    value = jnp.zeros((rows, extra), jnp.float32)
    for tick in range(ticks):
        ids = ids_ref[tick]
        blend = blend_ref[tick]
        mine = lane // (2 * experts) == tick
        for k in range(top):
            hit = jnp.logical_and(mine, expert == column(ids[k : k + 1]))
            value = value + jnp.where(hit, column(blend[k : k + 1]), 0.0)
    high = value.astype(jnp.bfloat16).astype(jnp.float32)
    low = value - high
    upper = (lane // experts) % 2 == 0
    out_ref[:, features:] = jnp.where(upper, high, low).astype(jnp.bfloat16)


def next_kernel(fed_ref, passed_ref, gain_ref, out_ref, state_ref):
    state = jnp.where(lax.axis_index("pipe") == 0, fed_ref[...].astype(jnp.float32), passed_ref[...].astype(jnp.float32))
    state_ref[...] = state.astype(jnp.bfloat16)
    out_ref[...] = rms(state, gain_ref[...])


def load_kernel(*refs):
    count = len(refs) // 2
    copies = [pltpu.make_async_copy(refs[i], refs[count + i], refs[-1].at[i]) for i in range(count)]
    for copy in copies:
        copy.start()
    for copy in copies:
        copy.wait()


def join_kernel(a_ref, b_ref, out_ref):
    rows = a_ref.shape[0]
    out_ref[:rows] = a_ref[...]
    out_ref[rows:] = b_ref[...]


def expert_kernel(tick, experts, pieces, *refs):
    blocks = refs[:pieces]
    refs = refs[pieces:]
    if tick:
        factor_ref, refs = refs[0], refs[1:]
        gate_ref, up_ref, down_ref, keep_ref, send_ref, rows_ref, inner_ref = refs
    else:
        gate_ref, up_ref, down_ref, keep_ref, send_ref, factor_ref, rows_ref, inner_ref = refs
    total, features = rows_ref.shape
    at = 0
    for block in blocks:
        count = block.shape[0]
        rows_ref[at : at + count] = block[:, :features]
        if not tick:
            factor_ref[at : at + count] = block[:, features:]
        at += count
    extra = factor_ref.shape[1]
    hidden = gate_ref.shape[1]
    step = min(256, total)
    wide = 256 if hidden % 256 == 0 else LANES
    tall = 512 if features % 512 == 0 else LANES
    half = total // 2

    @pl.loop(0, total // step)
    def _(part):
        span = pl.ds(pl.multiple_of(part * step, step), step)
        lane = lax.broadcasted_iota(jnp.int32, (step, extra), 1)
        wanted = jnp.logical_and(lane // (2 * experts) == tick, lane % experts == lax.axis_index("expert"))
        factor = jnp.sum(jnp.where(wanted, factor_ref[span].astype(jnp.float32), 0.0), axis=1, keepdims=True)
        rows = rows_ref[span]
        for tile in range(hidden // wide):
            cols = slice(tile * wide, (tile + 1) * wide)
            gate = jnp.dot(rows, gate_ref[:, cols], preferred_element_type=jnp.float32)
            up = jnp.dot(rows, up_ref[:, cols], preferred_element_type=jnp.float32)
            inner = gate / (1.0 + jnp.exp(-gate)) * up * factor
            inner_ref[span, cols] = inner.astype(jnp.bfloat16)

    for start, out_ref in ((0, keep_ref), (half, send_ref)):
        inner = inner_ref[start : start + half]
        for tile in range(features // tall):
            cols = slice(tile * tall, (tile + 1) * tall)
            out_ref[:, cols] = jnp.dot(inner, down_ref[:, cols], preferred_element_type=jnp.float32).astype(jnp.bfloat16)


def chip_kernel(keep_ref, got_ref, own_ref, side_ref, *far_refs):
    rows = own_ref.shape[0]
    total = keep_ref[...].astype(jnp.float32) + got_ref[...].astype(jnp.float32)
    own_ref[...] = total[:rows]
    side_ref[...] = total[rows : 2 * rows].astype(jnp.bfloat16)
    for j, far_ref in enumerate(far_refs):
        far_ref[...] = total[2 * rows * (j + 1) : 2 * rows * (j + 2)].astype(jnp.bfloat16)


def gather_kernel(count, x_ref, own_ref, side_ref, *refs):
    far_refs, (mine_ref, other_ref) = refs[:count], refs[count:]
    rows = x_ref.shape[0]
    total = far_refs[0][...].astype(jnp.float32)
    for far_ref in far_refs[1:]:
        total = total + far_ref[...].astype(jnp.float32)
    mine_ref[...] = x_ref[...].astype(jnp.float32) + own_ref[...] + side_ref[...].astype(jnp.float32) + total[:rows]
    other_ref[...] = total[rows:].astype(jnp.bfloat16)


def finish_kernel(mine_ref, got_ref, out_ref):
    out_ref[...] = (mine_ref[...] + got_ref[...].astype(jnp.float32)).astype(jnp.bfloat16)


def last_kernel(mine_ref, got_ref, *refs):
    earlier, out_ref = refs[:-1], refs[-1]
    for tick, ref in enumerate(earlier):
        out_ref[tick, 0] = ref[...]
    out_ref[len(earlier), 0] = (mine_ref[...] + got_ref[...].astype(jnp.float32)).astype(jnp.bfloat16)


def call(kernel, outs, *args, spec=VMEM, scratch=(), mib=8, cost=None):
    single = not isinstance(outs, (list, tuple))
    if spec is HBM:
        args = [pltpu.with_memory_space_constraint(arg, pltpu.HBM) for arg in args]
    return pl.pallas_call(
        kernel,
        out_shape=outs,
        in_specs=[spec] * len(args),
        out_specs=VMEM if single else [VMEM] * len(outs),
        scratch_shapes=list(scratch),
        compiler_params=params(mib),
        cost_estimate=cost and pl.CostEstimate(flops=cost, bytes_accessed=0, transcendentals=0),
    )(*args)


def shape(rows, columns, dtype=jnp.bfloat16):
    return jax.ShapeDtypeStruct((rows, columns), dtype)


def local(
    resident_batchlets,
    incoming_batchlets,
    segment_rms_gain,
    gating_projection,
    expanding_projection,
    contracting_projection,
    picked_specialist_ids,
    blend_factors,
):
    experts = lax.axis_size("expert")
    sections = lax.axis_size("pipe")
    plan = Plan(experts)
    rows, features = resident_batchlets.shape[1:]
    ticks = picked_specialist_ids.shape[0]
    extra = -(-2 * ticks * experts // LANES) * LANES
    weights = (gating_projection[0], expanding_projection[0], contracting_projection[0])
    hidden = weights[0].shape[1]
    total = rows * experts

    def move(value, perm):
        return lax.ppermute(value, "expert", perm)

    state = resident_batchlets[0]
    factors = None
    outputs = []
    for tick in range(ticks):
        if tick == 0:
            ids = jnp.swapaxes(picked_specialist_ids[:, 0], 1, 2)
            blend = jnp.swapaxes(blend_factors[:, 0], 1, 2)
            normed, state = call(
                functools.partial(first_kernel, experts),
                [shape(rows, features + extra), shape(rows, features)],
                state,
                segment_rms_gain,
                ids,
                blend,
                spec=HBM,
                scratch=[
                    pltpu.VMEM(segment_rms_gain.shape, jnp.float32),
                    pltpu.VMEM(ids.shape, jnp.int32),
                    pltpu.VMEM(blend.shape, jnp.float32),
                    pltpu.SemaphoreType.DMA((4,)),
                ],
            )
        else:
            passed = lax.ppermute(outputs[-1], "pipe", [(i, i + 1) for i in range(sections - 1)])
            normed, state = call(
                next_kernel,
                [shape(rows, features), shape(rows, features)],
                incoming_batchlets[tick - 1],
                passed,
                segment_rms_gain,
            )
        width = normed.shape[1]
        beside = move(normed, plan.side)
        partner = move(normed, plan.core)
        chip = call(join_kernel, shape(2 * rows, width), normed, partner)
        far = [move(chip, perm) for perm in plan.far]
        if tick == 0:
            weights = call(
                load_kernel,
                [shape(*w.shape) for w in weights],
                *weights,
                spec=HBM,
                scratch=[pltpu.SemaphoreType.DMA((3,))],
                cost=3000000000,
            )
        direct = [normed, beside] + far
        relayed = [partner] + [move(block, plan.core) for block in direct[1:]]
        blocks = direct + relayed
        outs = [shape(total // 2, features), shape(total // 2, features)]
        if tick == 0:
            outs.append(shape(total, extra))
        args = blocks + ([factors] if tick else []) + list(weights)
        got = call(
            functools.partial(expert_kernel, tick, experts, len(blocks)),
            outs,
            *args,
            scratch=[pltpu.VMEM((total, features), jnp.bfloat16), pltpu.VMEM((total, hidden), jnp.bfloat16)],
            mib=16,
        )
        keep, send = got[:2]
        if tick == 0:
            factors = got[2]
        swapped = move(send, plan.core)
        own, side, *far = call(
            chip_kernel,
            [shape(rows, features, jnp.float32), shape(rows, features)] + [shape(2 * rows, features)] * len(plan.back),
            keep,
            swapped,
        )
        far = [move(block, perm) for block, perm in reversed(list(zip(far, plan.back)))][::-1]
        side = move(side, plan.side)
        part, other = call(
            functools.partial(gather_kernel, len(far)),
            [shape(rows, features, jnp.float32), shape(rows, features)],
            state,
            own,
            side,
            *far,
        )
        other = move(other, plan.core)
        if tick + 1 < ticks:
            outputs.append(call(finish_kernel, shape(rows, features), part, other))
        else:
            return call(last_kernel, jax.ShapeDtypeStruct((ticks, 1, rows, features), jnp.bfloat16), part, other, *outputs)


def solution(mesh):
    in_specs = (
        P("pipe", "expert", None),
        P(None, "expert", None),
        P("pipe", None),
        P("expert", None, None),
        P("expert", None, None),
        P("expert", None, None),
        P(None, "pipe", "expert", None),
        P(None, "pipe", "expert", None),
    )
    out_specs = P(None, "pipe", "expert", None)
    return jax.shard_map(local, mesh=mesh, in_specs=in_specs, out_specs=out_specs, check_vma=False)
```
